32 devices in a mesh: group: 2 (over y), chan: 8 (over z, x), rec: 2 (over core).
Axes of the slice: x: 2, y: 2, z: 4, core: 2. Of those that a mesh axis runs over, the one named last changes fastest.
Arguments:
- records: bfloat16 [256, 128, 1024], P(('group', 'chan'), 'rec'), parts along dimension 0, may hold values from -50 to 50
- valid: int32 [256, 128], P(('group', 'chan'), 'rec'), parts along dimension 0, may hold values 0 or 1
- sources: int32 [16], P('group'), parts along dimension 0, may hold values from 0 to 127, as said below
Outputs:
- cross: float32 [256, 8, 1024], P(('group', 'chan'), None, 'rec'), parts along dimension 0
The draws below stay inside these ranges and needn't reach their ends.
There are 2 independent parts, one for each index of `group`. The reference program is written for one: setup_inputs(seed, part) draws one part's arguments, and reference() takes and returns one part's arrays. A program takes and returns all parts, laid end to end along the dimension named above; each array names one. Nothing has to cross between parts.
Inputs may be any that keep to these rules, and one draw needn't show every extreme that they name: `sources`: 8 distinct channel numbers.
All inputs are finite; a program needn't handle non-finite values. No bound on the sum of `valid` on one device may be relied on, other than what follows from the above.
Results may differ from the reference program's by a relative error of at most 0.0034.
Values may be sent and summed in bfloat16 or wider, within the bound.
No kernel may reach another device: no remote copies, remote signals or barrier semaphores. Data moves between devices by JAX's collectives and lax.ppermute only.
A program may use at most 64 MiB of HBM per device.

```python
import math
import jax
import jax.numpy as jnp
from jax import lax

CH_DEV = 16
L = 1024
S = 8
F = 512
CHANNELS = 128
RECORDS = 128


def draw_records(key, part):
    key_noise, key_scale = jax.random.split(jax.random.fold_in(key, 11))
    noise = jnp.clip(jax.random.normal(key_noise, (CHANNELS, RECORDS, L), jnp.float32), -5.0, 5.0)
    scale = jnp.exp(jax.random.uniform(key_scale, (CHANNELS, RECORDS, 1), jnp.float32, 0.0, math.log(10.0)))
    return (noise * scale).astype(jnp.bfloat16)


def draw_sources(key, part):
    order = jax.random.permutation(jax.random.fold_in(key, 23), CHANNELS)
    return order[:S].astype(jnp.int32)


def plant(array, rng, smallest, top_value):
    longest = array.shape.index(max(array.shape))
    spots = []
    for shift in (0, 1):
        where = [jax.random.randint(jax.random.fold_in(rng, axis), (), 0, length) for axis, length in enumerate(array.shape)]
        where[longest] = (where[longest] + shift) % array.shape[longest]
        spots.append(tuple(where))
    return array.at[spots[0]].set(smallest).at[spots[1]].set(top_value)


def setup_inputs(seed: int = 0, part: int = 0) -> dict:
    streams_of = jax.random.split(jax.random.key(seed), 4)
    own_keys = jax.random.split(jax.random.fold_in(streams_of[3], part), 4)
    records = draw_records(jax.random.fold_in(jax.random.fold_in(streams_of[3], part), 71), part)
    valid = plant((jax.random.randint(own_keys[1], (CHANNELS, RECORDS), 0, 4) < 3).astype(jnp.int32), jax.random.fold_in(own_keys[1], 1), 0, 1)
    sources = draw_sources(jax.random.fold_in(jax.random.fold_in(streams_of[3], part), 71), part)
    return {"records": records, "valid": valid, "sources": sources}


def dft_table(length, bins):
    times = jnp.arange(length, dtype=jnp.int32)[:, None]
    freqs = jnp.arange(bins, dtype=jnp.int32)[None, :]
    phase = (times * freqs % length).astype(jnp.float32) * (2.0 * math.pi / length)
    return jnp.concatenate([jnp.cos(phase), -jnp.sin(phase)], axis=1).astype(jnp.bfloat16)

def transform(rows, table):
    lead = rows.shape[:-1]
    flat = rows.reshape(-1, rows.shape[-1])
    return jnp.dot(flat, table, preferred_element_type=jnp.float32).reshape(lead + (table.shape[1],))

def whiten(spec, bins):
    real_part = spec[..., :bins]
    imag_part = spec[..., bins:]
    power = lax.optimization_barrier(jnp.mean(real_part * real_part + imag_part * imag_part, axis=-1, keepdims=True))
    return (spec * lax.rsqrt(power + 1e-06)).astype(jnp.bfloat16)

def stack_block(spec, wsrc, bins):
    hp = lax.Precision.HIGHEST
    xr = spec[..., :bins]
    xi = spec[..., bins:]
    wr = wsrc[..., :bins].astype(jnp.float32)
    wi = wsrc[..., bins:].astype(jnp.float32)
    real_sum = jnp.einsum('crf,srf->csf', xr, wr, precision=hp) + jnp.einsum('crf,srf->csf', xi, wi, precision=hp)
    imag_sum = jnp.einsum('crf,srf->csf', xi, wr, precision=hp) - jnp.einsum('crf,srf->csf', xr, wi, precision=hp)
    return jnp.concatenate([real_sum, imag_sum], axis=-1)

def reference(records, valid, sources):
    table = dft_table(L, F)
    masked = records * valid[:, :, None].astype(jnp.bfloat16)
    picked = masked[sources]
    wsrc = whiten(transform(picked, table), F)
    blocks = masked.reshape(CHANNELS // CH_DEV, CH_DEV, RECORDS, L)

    def one_block(rows):
        return stack_block(transform(rows, table), wsrc, F)
    result = lax.map(one_block, blocks)
    return result.reshape(CHANNELS, S, 2 * F) / RECORDS
```

```python
import functools
import math

import jax
import jax.numpy as jnp
import numpy as np
from jax import lax
from jax.experimental import pallas as pl
from jax.experimental.pallas import tpu as pltpu
from jax.sharding import PartitionSpec as P

VMEM = pl.BlockSpec(memory_space=pltpu.VMEM)
SMEM = pl.BlockSpec(memory_space=pltpu.SMEM)
LANES = 128
QUAD = 4
ROOM = pltpu.CompilerParams(vmem_limit_bytes=16 << 20)


def dft_table(length, bins):
    times = np.arange(length)[:, None]
    freqs = np.arange(bins)[None, :]
    phase = (times * freqs % length) * (2.0 * math.pi / length)
    table = np.concatenate([np.cos(phase), -np.sin(phase)], axis=1)
    return jnp.asarray(table.astype(np.float32).astype(jnp.bfloat16))


def row_mask(valid_row, start, rows):
    n = valid_row.shape[1]
    lane = lax.broadcasted_iota(jnp.int32, (rows, n), 1)
    row = lax.broadcasted_iota(jnp.int32, (rows, n), 0)
    hit = jnp.where(lane == row + start, valid_row.astype(jnp.float32), 0.0)
    return jnp.sum(hit, axis=1, keepdims=True)


def pick_kernel(sources, valid, records, *outs):
    per_dev, rec_rows, _ = records.shape
    block = rec_rows // QUAD
    me = lax.axis_index("chan")
    quad = lax.rem(me, QUAD)
    for s in range(sources.shape[0]):
        local = sources[s] - me * per_dev
        owned = jnp.logical_and(local >= 0, local < per_dev)

        @pl.when(owned)
        def _():
            row = valid[pl.ds(local, 1), :]
            for j, out in enumerate(outs):
                start = pl.multiple_of((quad ^ j) * block, block)
                part = records[local, pl.ds(start, block), :].astype(jnp.float32)
                out[s] = (part * row_mask(row, start, block)).astype(out.dtype)

        @pl.when(jnp.logical_not(owned))
        def _():
            for out in outs:
                out[s] = jnp.zeros(out.shape[1:], out.dtype)


def pick(sources, valid, records):
    n_src = sources.shape[0]
    _, rec_rows, length = records.shape
    part = jax.ShapeDtypeStruct((n_src, rec_rows // QUAD, length), records.dtype)
    return pl.pallas_call(
        pick_kernel,
        out_shape=(part,) * QUAD,
        in_specs=[SMEM, VMEM, VMEM],
        out_specs=(VMEM,) * QUAD,
        compiler_params=ROOM,
        name="pick",
    )(sources, valid, records)


def spectra_kernel(valid, table, records, out):
    chans, rec_rows, length = records.shape
    step = pl.program_id(0)
    flat = records[...].reshape(chans * rec_rows, length)
    spec = jnp.dot(flat, table[...], preferred_element_type=jnp.float32)
    for c in range(chans):
        mask = row_mask(valid[pl.ds(step * chans + c, 1), :], 0, rec_rows)
        part = spec[c * rec_rows : (c + 1) * rec_rows] * mask
        for f in range(out.shape[0]):
            out[f, c] = part[:, f * LANES : (f + 1) * LANES]


def spectra_of(valid, table, records, chans=2):
    per_dev, rec_rows, length = records.shape
    width = table.shape[1]
    return pl.pallas_call(
        spectra_kernel,
        out_shape=jax.ShapeDtypeStruct((width // LANES, per_dev, rec_rows, LANES), jnp.float32),
        grid=(per_dev // chans,),
        in_specs=[
            VMEM,
            VMEM,
            pl.BlockSpec((chans, rec_rows, length), lambda i: (i, 0, 0)),
        ],
        out_specs=pl.BlockSpec(
            (width // LANES, chans, rec_rows, LANES), lambda i: (0, i, 0, 0)
        ),
        cost_estimate=pl.CostEstimate(
            flops=2 * per_dev * rec_rows * length * width,
            bytes_accessed=per_dev * rec_rows * (2 * length + 4 * width),
            transcendentals=0,
        ),
        compiler_params=ROOM,
        name="spectra",
    )(valid, table, records)


def whiten_kernel(table, mine, other, out, mixed):
    n_src, block, length = mine.shape
    bins = table.shape[1] // 2
    rows = (mine[...] + other[...]).reshape(n_src * block, length)
    spec = jnp.dot(rows, table[...], preferred_element_type=jnp.float32)
    real, imag = spec[:, :bins], spec[:, bins:]
    power = jnp.sum(real * real + imag * imag, axis=1, keepdims=True) / bins
    white = spec * lax.rsqrt(power + 1e-06)
    for f in range(0, 2 * bins, LANES):
        for s in range(n_src):
            part = white[s * block : (s + 1) * block, f : f + LANES]
            mixed[f // LANES, pl.ds(s, block, stride=n_src), :] = part
        out[:, f : f + LANES] = mixed[f // LANES].astype(out.dtype)


def whitened_of(table, mine, other):
    n_src, block, _ = mine.shape
    width = table.shape[1]
    rows = n_src * block
    return pl.pallas_call(
        whiten_kernel,
        out_shape=jax.ShapeDtypeStruct((rows, width), jnp.bfloat16),
        in_specs=[VMEM, VMEM, VMEM],
        out_specs=VMEM,
        scratch_shapes=[pltpu.VMEM((width // LANES, rows, LANES), jnp.float32)],
        compiler_params=ROOM,
        name="whiten",
    )(table, mine, other)


def cross_kernel(other, mode, first, spectra, white, *rest):
    both = mode == "both"
    acc, out, conj = (None, *rest) if first else rest
    chans = spectra.shape[1]
    rows, width = white.shape
    n_src = out.shape[-2]
    block = rows // n_src
    bins = width // 2
    quad = lax.rem(lax.axis_index("chan"), QUAD)
    base = (quad ^ other) * block
    core = lax.axis_index("rec")
    part = core if mode == "keep" else 1 - core
    tiles = bins // LANES
    for f in range(tiles):
        real = white[:, f * LANES : (f + 1) * LANES].astype(jnp.float32)
        imag = white[:, bins + f * LANES : bins + (f + 1) * LANES].astype(jnp.float32)
        conj[0, f] = real if both else jnp.where(part == 0, real, -imag)
        conj[1, f] = imag if both else jnp.where(part == 0, imag, real)
    group = 8 if both else chans

    @pl.loop(0, tiles)
    def _(f):
        lo = pl.multiple_of(f * LANES, LANES)
        for c0 in range(0, chans, group):
            names = range(c0, c0 + group)
            if both:
                spots_of = [(p, c) for c in names for p in (0, 1)]
            else:
                spots_of = [(part, c) for c in names]
            if first:
                sums = [jnp.zeros((n_src, LANES), jnp.float32) for _ in spots_of]
            else:
                sums = [acc[p, c, :, pl.ds(lo, LANES)] for p, c in spots_of]

            def add(r, sums):
                a = conj[0, f, pl.ds(r * n_src, n_src), :]
                b = conj[1, f, pl.ds(r * n_src, n_src), :]
                new = []
                for i, c in enumerate(names):
                    xr = spectra[f, c, pl.ds(base + r, 1), :]
                    xi = spectra[tiles + f, c, pl.ds(base + r, 1), :]
                    if both:
                        new.append(sums[2 * i] + (xr * a + xi * b))
                        new.append(sums[2 * i + 1] + (xi * a - xr * b))
                    else:
                        new.append(sums[i] + (xr * a + xi * b))
                return new

            for r in range(block):
                sums = add(r, sums)
            for (p, c), total in zip(spots_of, sums):
                if both:
                    out[p, c, :, pl.ds(lo, LANES)] = total
                else:
                    out[c, :, pl.ds(lo, LANES)] = total


def cross_of(spectra, white, n_src, other, mode, acc=None):
    both = mode == "both"
    chans = spectra.shape[1]
    rows, width = white.shape
    bins = width // 2
    shape = (2, chans, n_src, bins) if both else (chans, n_src, bins)
    args = (spectra, white) + (() if acc is None else (acc,))
    parts = 2 if both else 1
    return pl.pallas_call(
        functools.partial(cross_kernel, other, mode, acc is None),
        out_shape=jax.ShapeDtypeStruct(shape, jnp.float32),
        in_specs=[VMEM] * len(args),
        out_specs=VMEM,
        scratch_shapes=[pltpu.VMEM((2, bins // LANES, rows, LANES), jnp.float32)],
        input_output_aliases={2: 0} if both and acc is not None else {},
        cost_estimate=pl.CostEstimate(
            flops=4 * parts * chans * rows * bins * 16,
            bytes_accessed=rows * chans * width,
            transcendentals=0,
        ),
        compiler_params=ROOM,
        name="cross_" + mode,
    )(*args)


def per_device(records, valid, sources):
    per_dev, rec_rows, length = records.shape
    bins = length // 2
    n_src = sources.shape[0]
    n_chan = lax.axis_size("chan")
    n_rec = lax.axis_size("rec")
    table = dft_table(length, bins)

    def swap(value, bit):
        return lax.ppermute(value, "chan", [(i, i ^ bit) for i in range(n_chan)])

    picked = pick(sources, valid, records)
    arrived = [swap(picked[j], j) for j in (3, 1, 2)]
    spectra = spectra_of(valid, table, records)
    *arrived, spectra = lax.optimization_barrier((*arrived, spectra))
    home = picked[0] + arrived[0] + arrived[1] + arrived[2]
    bit = QUAD
    while bit * 2 < n_chan:
        home = home + swap(home, bit)
        bit *= 2
    white = whitened_of(table, home, swap(home, bit))
    others = [(j, swap(white, j)) for j in (1, 2, 3)]

    acc = cross_of(spectra, white, n_src, 0, "both")
    for j, block in others[:2]:
        acc = cross_of(spectra, block, n_src, j, "both", acc)
    j, block = others[2]
    send = cross_of(spectra, block, n_src, j, "send", acc)
    came = lax.ppermute(send, "rec", [(i, i ^ 1) for i in range(n_rec)])
    keep = cross_of(spectra, block, n_src, j, "keep", acc)
    return (keep + came) / (rec_rows * n_rec)


def solution(mesh):
    placed = (P(("group", "chan"), "rec", None), P(("group", "chan"), "rec"), P("group"))
    return jax.shard_map(
        per_device,
        mesh=mesh,
        in_specs=placed,
        out_specs=P(("group", "chan"), None, "rec"),
        check_vma=False,
    )
```

```python
import functools
import math

import jax
import jax.numpy as jnp
import numpy as np
from jax import lax
from jax.experimental import pallas as pl
from jax.experimental.pallas import tpu as pltpu
from jax.sharding import PartitionSpec as P


VMEM = pl.BlockSpec(memory_space=pltpu.VMEM)
SMEM = pl.BlockSpec(memory_space=pltpu.SMEM)
LANES = 128
QUAD = 4
STREAMS = 2
ROOM = pltpu.CompilerParams(vmem_limit_bytes=16 << 20)


def dft_table(length, bins):
    times = np.arange(length)[:, None]
    freqs = np.arange(bins)[None, :]
    phase = (times * freqs % length) * (2.0 * math.pi / length)
    table = np.concatenate([np.cos(phase), -np.sin(phase)], axis=1)
    return jnp.asarray(table.astype(np.float32).astype(jnp.bfloat16))


def row_mask(valid_row, start, rows):
    n = valid_row.shape[1]
    lane = lax.broadcasted_iota(jnp.int32, (rows, n), 1)
    row = lax.broadcasted_iota(jnp.int32, (rows, n), 0)
    hit = jnp.where(lane == row + start, valid_row.astype(jnp.float32), 0.0)
    return jnp.sum(hit, axis=1, keepdims=True)


def owner_of(sources, per_dev, s):
    owner = sources[s] // per_dev
    rank = jnp.int32(0)
    for before in range(s):
        rank += (sources[before] // per_dev == owner).astype(jnp.int32)
    return owner, rank


def pick_kernel(sources, valid, records, *rest):
    outs, (which, usable, buf, sems) = rest[: 2 * QUAD], rest[2 * QUAD :]
    per_dev, rec_rows, _ = records.shape
    n_src = sources.shape[0]
    room = outs[0].shape[0]
    block = rec_rows // QUAD
    me = lax.axis_index("chan")
    quad = lax.rem(me, QUAD)
    get_sources = pltpu.make_async_copy(sources, which, sems.at[n_src])
    get_valid = pltpu.make_async_copy(valid, usable, sems.at[n_src + 1])
    get_sources.start()
    get_valid.start()
    get_sources.wait()

    def copy(s):
        local = which[s] - me * per_dev
        return pltpu.make_async_copy(records.at[local], buf.at[s], sems.at[s])

    for s in range(n_src):

        @pl.when(owner_of(which, per_dev, s)[0] == me)
        def _():
            copy(s).start()

    get_valid.wait()
    for s in range(n_src):
        owner, rank = owner_of(which, per_dev, s)

        @pl.when(owner == me)
        def _():
            copy(s).wait()
            row = usable[pl.ds(which[s] - me * per_dev, 1), :]
            for other in range(QUAD):
                start = pl.multiple_of((quad ^ other) * block, block)
                rows = buf[s, pl.ds(start, block), :].astype(jnp.float32)
                rows = (rows * row_mask(row, start, block)).astype(buf.dtype)

                @pl.when(rank < room)
                def _():
                    outs[other][jnp.minimum(rank, room - 1)] = rows

                @pl.when(rank >= room)
                def _():
                    outs[QUAD + other][jnp.maximum(rank - room, 0)] = rows


def pick(sources, valid, records, room):
    n_src = sources.shape[0]
    _, rec_rows, length = records.shape
    parts = [
        jax.ShapeDtypeStruct((count, rec_rows // QUAD, length), records.dtype)
        for count in (room, n_src - room)
    ]
    args = [pltpu.with_memory_space_constraint(x, pltpu.HBM) for x in (sources, valid, records)]
    return pl.pallas_call(
        pick_kernel,
        out_shape=(parts[0],) * QUAD + (parts[1],) * QUAD,
        in_specs=[pl.BlockSpec(memory_space=pltpu.HBM)] * 3,
        out_specs=(VMEM,) * (2 * QUAD),
        scratch_shapes=[
            pltpu.SMEM(sources.shape, sources.dtype),
            pltpu.VMEM(valid.shape, valid.dtype),
            pltpu.VMEM((n_src, rec_rows, length), records.dtype),
            pltpu.SemaphoreType.DMA((n_src + 2,)),
        ],
        compiler_params=ROOM,
        name="pick",
    )(*args)


def merge_kernel(per_dev, sources, *refs):
    firsts, others, outs = refs[:QUAD], refs[QUAD : 2 * QUAD], refs[2 * QUAD :]
    room = firsts[0].shape[0]
    part = outs[0].shape[1]
    me = lax.axis_index("chan")
    for s in range(sources.shape[0]):
        owner, rank = owner_of(sources, per_dev, s)
        near = owner // QUAD == me // QUAD

        def put(rows):
            for t, out in enumerate(outs):
                out[s] = rows[t * part : (t + 1) * part]

        @pl.when(jnp.logical_not(near))
        def _():
            for out in outs:
                out[s] = jnp.zeros(out.shape[1:], out.dtype)

        for j in range(QUAD):
            here = jnp.logical_and(near, lax.rem(owner, QUAD) ^ lax.rem(me, QUAD) == j)

            @pl.when(jnp.logical_and(here, rank < room))
            def _():
                put(firsts[j][jnp.minimum(rank, room - 1)])

            @pl.when(jnp.logical_and(here, rank >= room))
            def _():
                put(others[j][jnp.maximum(rank - room, 0)])


def merge(sources, per_dev, firsts, others):
    n_src = sources.shape[0]
    _, block, length = firsts[0].shape
    part = jax.ShapeDtypeStruct((n_src, block // STREAMS, length), firsts[0].dtype)
    return pl.pallas_call(
        functools.partial(merge_kernel, per_dev),
        out_shape=(part,) * STREAMS,
        in_specs=[SMEM] + [VMEM] * (2 * QUAD),
        out_specs=(VMEM,) * STREAMS,
        compiler_params=ROOM,
        name="merge",
    )(sources, *firsts, *others)


def spectra_kernel(chans, valid, table, records, out, buf, sems):
    per_dev, rec_rows, length = records.shape

    def copy(c0):
        part = pl.ds(c0, chans)
        return pltpu.make_async_copy(records.at[part], buf.at[part], sems.at[c0 // chans])

    for c0 in range(0, min(2 * chans, per_dev), chans):
        copy(c0).start()
    for c0 in range(0, per_dev, chans):
        copy(c0).wait()
        if c0 + 2 * chans < per_dev:
            copy(c0 + 2 * chans).start()
        flat = buf[c0 : c0 + chans].reshape(chans * rec_rows, length)
        spec = jnp.dot(flat, table[...], preferred_element_type=jnp.float32)
        for c in range(chans):
            mask = row_mask(valid[c0 + c : c0 + c + 1, :], 0, rec_rows)
            part = spec[c * rec_rows : (c + 1) * rec_rows] * mask
            for f in range(out.shape[0]):
                out[f, c0 + c] = part[:, f * LANES : (f + 1) * LANES]


def spectra_of(valid, table, records):
    per_dev, rec_rows, length = records.shape
    width = table.shape[1]
    chans = math.gcd(per_dev, 4)
    records = pltpu.with_memory_space_constraint(records, pltpu.HBM)
    return pl.pallas_call(
        functools.partial(spectra_kernel, chans),
        out_shape=jax.ShapeDtypeStruct((width // LANES, per_dev, rec_rows, LANES), jnp.float32),
        in_specs=[VMEM, VMEM, pl.BlockSpec(memory_space=pltpu.HBM)],
        out_specs=VMEM,
        scratch_shapes=[
            pltpu.VMEM(records.shape, records.dtype),
            pltpu.SemaphoreType.DMA((per_dev // chans,)),
        ],
        cost_estimate=pl.CostEstimate(
            flops=2 * per_dev * rec_rows * length * width,
            bytes_accessed=per_dev * rec_rows * (2 * length + 4 * width),
            transcendentals=0,
        ),
        compiler_params=ROOM,
        name="spectra",
    )(valid, table, records)


def whiten_kernel(table, mine, other, out, mixed):
    n_src, block, length = mine.shape
    bins = table.shape[1] // 2
    rows = (mine[...] + other[...]).reshape(n_src * block, length)
    spec = jnp.dot(rows, table[...], preferred_element_type=jnp.float32)
    real, imag = spec[:, :bins], spec[:, bins:]
    power = jnp.sum(real * real + imag * imag, axis=1, keepdims=True) / bins
    white = spec * lax.rsqrt(power + 1e-06)
    for f in range(0, 2 * bins, LANES):
        for s in range(n_src):
            part = white[s * block : (s + 1) * block, f : f + LANES]
            mixed[f // LANES, pl.ds(s, block, stride=n_src), :] = part
        out[:, f : f + LANES] = mixed[f // LANES].astype(out.dtype)


def whitened_of(table, mine, other):
    n_src, block, _ = mine.shape
    width = table.shape[1]
    rows = n_src * block
    return pl.pallas_call(
        whiten_kernel,
        out_shape=jax.ShapeDtypeStruct((rows, width), jnp.bfloat16),
        in_specs=[VMEM, VMEM, VMEM],
        out_specs=VMEM,
        scratch_shapes=[pltpu.VMEM((width // LANES, rows, LANES), jnp.float32)],
        compiler_params=ROOM,
        name="whiten",
    )(table, mine, other)


def cross_kernel(places, mode, first, spectra, *rest):
    both = mode == "both"
    whites, rest = rest[: len(places)], rest[len(places) :]
    acc, out, conj = (None, *rest) if first else rest
    chans, rec_rows = spectra.shape[1:3]
    width = whites[0].shape[1]
    n_src = out.shape[-2]
    part_rows = rec_rows // (QUAD * STREAMS)
    bins = width // 2
    tiles = bins // LANES
    quad = lax.rem(lax.axis_index("chan"), QUAD)
    core = lax.axis_index("rec")
    part = core if mode == "keep" else 1 - core
    for k, white in enumerate(whites):
        for f in range(tiles):
            real = white[:, f * LANES : (f + 1) * LANES].astype(jnp.float32)
            imag = white[:, bins + f * LANES : bins + (f + 1) * LANES].astype(jnp.float32)
            conj[k, 0, f] = real if both else jnp.where(part == 0, real, -imag)
            conj[k, 1, f] = imag if both else jnp.where(part == 0, imag, real)
    group = 8 if both else chans

    @pl.loop(0, tiles)
    def _(f):
        lo = pl.multiple_of(f * LANES, LANES)
        for c0 in range(0, chans, group):
            names = range(c0, c0 + group)
            if both:
                spots = [(p, c) for c in names for p in (0, 1)]
            else:
                spots = [(part, c) for c in names]
            if first:
                sums = [jnp.zeros((n_src, LANES), jnp.float32) for _ in spots]
            else:
                sums = [acc[p, c, :, pl.ds(lo, LANES)] for p, c in spots]
            for k, (other, stream) in enumerate(places):
                base = ((quad ^ other) * STREAMS + stream) * part_rows
                for r in range(part_rows):
                    a = conj[k, 0, f, r * n_src : (r + 1) * n_src, :]
                    b = conj[k, 1, f, r * n_src : (r + 1) * n_src, :]
                    for i, c in enumerate(names):
                        xr = spectra[f, c, pl.ds(base + r, 1), :]
                        xi = spectra[tiles + f, c, pl.ds(base + r, 1), :]
                        if both:
                            sums[2 * i] += xr * a + xi * b
                            sums[2 * i + 1] += xi * a - xr * b
                        else:
                            sums[i] += xr * a + xi * b
            for (p, c), total in zip(spots, sums):
                if both:
                    out[p, c, :, pl.ds(lo, LANES)] = total
                else:
                    out[c, :, pl.ds(lo, LANES)] = total.astype(out.dtype)


def cross_of(spectra, blocks, n_src, mode="both", acc=None):
    places, whites = zip(*blocks)
    chans = spectra.shape[1]
    rows, width = whites[0].shape
    bins = width // 2
    both = mode == "both"
    shape = (2, chans, n_src, bins) if both else (chans, n_src, bins)
    args = (spectra, *whites) + (() if acc is None else (acc,))
    return pl.pallas_call(
        functools.partial(cross_kernel, places, mode, acc is None),
        out_shape=jax.ShapeDtypeStruct(shape, jnp.bfloat16 if mode == "send" else jnp.float32),
        in_specs=[VMEM] * len(args),
        out_specs=VMEM,
        scratch_shapes=[pltpu.VMEM((len(places), 2, bins // LANES, rows, LANES), jnp.float32)],
        input_output_aliases={len(args) - 1: 0} if both and acc is not None else {},
        cost_estimate=pl.CostEstimate(
            flops=4 * (2 if both else 1) * chans * rows * bins * len(places) * 16,
            bytes_accessed=rows * chans * width * len(places),
            transcendentals=0,
        ),
        compiler_params=ROOM,
    )(*args)


def stacks(records, valid, sources):
    per_dev, rec_rows, length = records.shape
    bins = length // 2
    n_src = sources.shape[0]
    n_chan = lax.axis_size("chan")
    n_rec = lax.axis_size("rec")
    table = dft_table(length, bins)

    def swap(value, bit):
        return lax.ppermute(value, "chan", [(i, i ^ bit) for i in range(n_chan)])

    room = n_src // 2
    picked = pick(sources, valid, records, room)
    first, more = picked[:QUAD], picked[QUAD:]
    came = {j: swap(first[j], j) for j in (3, 1, 2)}
    owners = sources // per_dev
    held = jnp.sum(owners[:, None] == owners[None, :], axis=1)

    def scatter_more(parts):
        return [lax.ppermute(x, "chan", [(i, i ^ (j + 1)) for i in range(n_chan)]) for j, x in enumerate(parts)]

    rest = lax.cond(jnp.max(held) > room, scatter_more, lambda parts: parts, list(more[1:]))
    parts = merge(sources, per_dev, [first[0], came[1], came[2], came[3]], [more[0], *rest])
    last = n_chan // 2
    homes = []
    for t in range(STREAMS):
        home = parts[t]
        bit = QUAD
        while bit < last:
            home = home + swap(home, bit)
            bit *= 2
        homes.append((home, swap(home, last)))
    spectra = spectra_of(valid, table, records)
    acc = None
    gathered = []
    for t in range(STREAMS):
        home, other = homes[t]
        white = whitened_of(table, home, other)
        blocks = [((0, t), white)]
        for j in (3, 1, 2):
            blocks.append(((j, t), swap(white, j)))
        gathered.append(blocks)
        acc = cross_of(spectra, gathered[t][:1], n_src, "both", acc)
    for t in range(STREAMS):
        mine, *near, far = gathered[t]
        for block in near:
            acc = cross_of(spectra, [block], n_src, "both", acc)
        if t < STREAMS - 1:
            acc = cross_of(spectra, [far], n_src, "both", acc)
    send = cross_of(spectra, [far], n_src, "send", acc)
    came = lax.ppermute(send, "rec", [(i, i ^ 1) for i in range(n_rec)])
    keep = cross_of(spectra, [far], n_src, "keep", acc)
    return (keep + came.astype(jnp.float32)) / (rec_rows * n_rec)


def solution(mesh):
    placed = (P(("group", "chan"), "rec", None), P(("group", "chan"), "rec"), P("group"))
    return jax.shard_map(
        stacks,
        mesh=mesh,
        in_specs=placed,
        out_specs=P(("group", "chan"), None, "rec"),
        check_vma=False,
    )
```

```python
import functools
import math

import jax
import jax.numpy as jnp
import numpy as np
from jax import lax
from jax.experimental import pallas as pl
from jax.experimental.pallas import tpu as pltpu
from jax.sharding import PartitionSpec as P


VMEM = pl.BlockSpec(memory_space=pltpu.VMEM)
SMEM = pl.BlockSpec(memory_space=pltpu.SMEM)
LANES = 128
QUAD = 4
STREAMS = 2
ROOM = pltpu.CompilerParams(vmem_limit_bytes=16 << 20)


def dft_table(length, bins):
    times = np.arange(length)[:, None]
    freqs = np.arange(bins)[None, :]
    phase = (times * freqs % length) * (2.0 * math.pi / length)
    table = np.concatenate([np.cos(phase), -np.sin(phase)], axis=1)
    return jnp.asarray(table.astype(np.float32).astype(jnp.bfloat16))


def row_mask(valid_row, start, rows):
    n = valid_row.shape[1]
    lane = lax.broadcasted_iota(jnp.int32, (rows, n), 1)
    row = lax.broadcasted_iota(jnp.int32, (rows, n), 0)
    hit = jnp.where(lane == row + start, valid_row.astype(jnp.float32), 0.0)
    return jnp.sum(hit, axis=1, keepdims=True)


def owner_of(sources, per_dev, s):
    owner = lax.div(sources[s], per_dev)
    rank = jnp.int32(0)
    for before in range(s):
        rank += (lax.div(sources[before], per_dev) == owner).astype(jnp.int32)
    return owner, rank


def plan_kernel(per_dev, room, packed, sources, plan):
    n_src = sources.shape[0]
    rounds = 2 * QUAD * room
    me = lax.axis_index("chan")
    for i in range(rounds):
        plan[i] = jnp.int32(-1)
    owners = [lax.div(sources[s], per_dev) for s in range(n_src)]
    quads = [lax.div(owner, QUAD) for owner in owners]
    crowded = jnp.int32(0)
    counts = [jnp.int32(0), jnp.int32(0)]
    for s in range(n_src):
        rank = jnp.int32(0)
        for before in range(s):
            rank += (owners[before] == owners[s]).astype(jnp.int32)
        crowded = jnp.maximum(crowded, rank + 1)
        place = jnp.int32(s)
        if packed:
            place = jnp.where(quads[s] == 0, counts[0], n_src - 1 - counts[1])
            counts[0] += (quads[s] == 0).astype(jnp.int32)
            counts[1] += (quads[s] != 0).astype(jnp.int32)
        plan[rounds + place] = jnp.int32(s)
        later = (rank >= room).astype(jnp.int32)
        member = lax.rem(owners[s], QUAD) ^ lax.rem(me, QUAD)

        @pl.when(quads[s] == lax.div(me, QUAD))
        def _():
            plan[(later * QUAD + member) * room + rank - later * room] = place

    plan[rounds + n_src] = (crowded > room).astype(jnp.int32)
    most = jnp.maximum(counts[0], counts[1])
    plan[rounds + n_src + 1] = (most > n_src - spare_of(n_src)).astype(jnp.int32)


def spare_of(n_src):
    return n_src // 4


def plan_of(sources, per_dev, room, packed):
    size = 2 * QUAD * room + sources.shape[0] + 2
    return pl.pallas_call(
        functools.partial(plan_kernel, per_dev, room, packed),
        out_shape=jax.ShapeDtypeStruct((size,), jnp.int32),
        in_specs=[SMEM],
        out_specs=SMEM,
        compiler_params=ROOM,
        name="plan",
    )(sources)


def pick_kernel(sources, valid, records, *rest):
    outs, (which, usable, buf, sems) = rest[: 2 * QUAD], rest[2 * QUAD :]
    per_dev, rec_rows, _ = records.shape
    n_src = sources.shape[0]
    room = outs[0].shape[0]
    block = rec_rows // QUAD
    me = lax.axis_index("chan")
    quad = lax.rem(me, QUAD)
    get_sources = pltpu.make_async_copy(sources, which, sems.at[n_src])
    get_valid = pltpu.make_async_copy(valid, usable, sems.at[n_src + 1])
    get_sources.start()
    get_valid.start()
    get_sources.wait()

    def copy(s):
        local = which[s] - me * per_dev
        return pltpu.make_async_copy(records.at[local], buf.at[s], sems.at[s])

    for s in range(n_src):

        @pl.when(owner_of(which, per_dev, s)[0] == me)
        def _():
            copy(s).start()

    get_valid.wait()
    for s in range(n_src):
        owner, rank = owner_of(which, per_dev, s)

        @pl.when(owner == me)
        def _():
            copy(s).wait()
            row = usable[pl.ds(which[s] - me * per_dev, 1), :]
            for other in range(QUAD):
                start = pl.multiple_of((quad ^ other) * block, block)
                rows = buf[s, pl.ds(start, block), :].astype(jnp.float32)
                rows = (rows * row_mask(row, start, block)).astype(buf.dtype)

                @pl.when(rank < room)
                def _():
                    outs[other][jnp.minimum(rank, room - 1)] = rows

                @pl.when(rank >= room)
                def _():
                    outs[QUAD + other][jnp.maximum(rank - room, 0)] = rows


def pick(sources, valid, records, room):
    n_src = sources.shape[0]
    _, rec_rows, length = records.shape
    parts = [
        jax.ShapeDtypeStruct((count, rec_rows // QUAD, length), records.dtype)
        for count in (room, n_src - room)
    ]
    args = [pltpu.with_memory_space_constraint(x, pltpu.HBM) for x in (sources, valid, records)]
    return pl.pallas_call(
        pick_kernel,
        out_shape=(parts[0],) * QUAD + (parts[1],) * QUAD,
        in_specs=[pl.BlockSpec(memory_space=pltpu.HBM)] * 3,
        out_specs=(VMEM,) * (2 * QUAD),
        scratch_shapes=[
            pltpu.SMEM(sources.shape, sources.dtype),
            pltpu.VMEM(valid.shape, valid.dtype),
            pltpu.VMEM((n_src, rec_rows, length), records.dtype),
            pltpu.SemaphoreType.DMA((n_src + 2,)),
        ],
        compiler_params=ROOM,
        name="pick",
    )(*args)


def merge_kernel(spare, plan, *refs):
    parts, outs = refs[: 2 * QUAD], refs[2 * QUAD :]
    room = parts[0].shape[0]
    n_src, rows = outs[0].shape[:2]
    upper = lax.rem(lax.div(lax.axis_index("chan"), QUAD), 2) == 1
    for out in outs:
        out[...] = jnp.zeros(out.shape, out.dtype)

    def put(block, place):
        for t in range(STREAMS):
            half = block[t * rows : (t + 1) * rows]
            outs[t][place] = half
            if not spare:
                continue
            sent, left = outs[STREAMS + t], outs[2 * STREAMS + t]
            depth = jnp.where(upper, place - spare, place)
            fits = jnp.logical_and(depth >= 0, depth < n_src - spare)

            @pl.when(fits)
            def _():
                sent[jnp.clip(depth, 0, n_src - spare - 1)] = half

            @pl.when(jnp.logical_not(fits))
            def _():
                left[jnp.where(upper, place, place - n_src + spare)] = half

    def put_round(later):
        for j in range(QUAD):
            for k in range(room):
                place = plan[(later * QUAD + j) * room + k]

                @pl.when(place >= 0)
                def _():
                    put(parts[later * QUAD + j][k], place)

    put_round(0)

    @pl.when(plan[2 * QUAD * room + n_src] == 1)
    def _():
        put_round(1)


def merge(plan, n_src, spare, parts):
    _, block, length = parts[0].shape
    dtype = parts[0].dtype
    sizes = [n_src, n_src - spare, spare] if spare else [n_src]
    return pl.pallas_call(
        functools.partial(merge_kernel, spare),
        out_shape=[
            jax.ShapeDtypeStruct((size, block // STREAMS, length), dtype)
            for size in sizes
            for _ in range(STREAMS)
        ],
        in_specs=[SMEM] + [VMEM] * (2 * QUAD),
        out_specs=[VMEM] * (len(sizes) * STREAMS),
        compiler_params=ROOM,
        name="merge",
    )(plan, *parts)


def spectra_kernel(chans, valid, table, records, out, buf, sems):
    per_dev, rec_rows, length = records.shape

    def copy(c0):
        part = pl.ds(c0, chans)
        return pltpu.make_async_copy(records.at[part], buf.at[part], sems.at[c0 // chans])

    for c0 in range(0, min(2 * chans, per_dev), chans):
        copy(c0).start()
    for c0 in range(0, per_dev, chans):
        copy(c0).wait()
        if c0 + 2 * chans < per_dev:
            copy(c0 + 2 * chans).start()
        flat = buf[c0 : c0 + chans].reshape(chans * rec_rows, length)
        spec = jnp.dot(flat, table[...], preferred_element_type=jnp.float32)
        for c in range(chans):
            mask = row_mask(valid[c0 + c : c0 + c + 1, :], 0, rec_rows)
            part = spec[c * rec_rows : (c + 1) * rec_rows] * mask
            for f in range(out.shape[0]):
                out[f, c0 + c] = part[:, f * LANES : (f + 1) * LANES]


def spectra_of(valid, table, records):
    per_dev, rec_rows, length = records.shape
    width = table.shape[1]
    chans = math.gcd(per_dev, 4)
    records = pltpu.with_memory_space_constraint(records, pltpu.HBM)
    return pl.pallas_call(
        functools.partial(spectra_kernel, chans),
        out_shape=jax.ShapeDtypeStruct((width // LANES, per_dev, rec_rows, LANES), jnp.float32),
        in_specs=[VMEM, VMEM, pl.BlockSpec(memory_space=pltpu.HBM)],
        out_specs=VMEM,
        scratch_shapes=[
            pltpu.VMEM(records.shape, records.dtype),
            pltpu.SemaphoreType.DMA((per_dev // chans,)),
        ],
        cost_estimate=pl.CostEstimate(
            flops=2 * per_dev * rec_rows * length * width,
            bytes_accessed=per_dev * rec_rows * (2 * length + 4 * width),
            transcendentals=0,
        ),
        compiler_params=ROOM,
        name="spectra",
    )(valid, table, records)


def whiten_kernel(spare, plan, table, mine, *rest):
    (*came, out, mixed, rows) = rest
    n_src, block, length = mine.shape
    bins = table.shape[1] // 2
    base = plan.shape[0] - 2 - n_src
    upper = lax.rem(lax.div(lax.axis_index("chan"), QUAD), 2) == 1

    def arrived(place, high):
        if not spare:
            return came[0][place]
        if high:
            first, second = place, place - n_src + spare
        else:
            first, second = place - spare, place
        fits = 0 <= first < n_src - spare
        return came[0][first] if fits else came[1][second]

    for high in (False, True):

        @pl.when(upper == high)
        def _():
            for place in range(n_src):
                rows[plan[base + place]] = mine[place] + arrived(place, high)

    spec = jnp.dot(
        rows[...].reshape(n_src * block, length),
        table[...],
        preferred_element_type=jnp.float32,
    )
    real, imag = spec[:, :bins], spec[:, bins:]
    power = jnp.sum(real * real + imag * imag, axis=1, keepdims=True) / bins
    white = spec * lax.rsqrt(power + 1e-06)
    for f in range(0, 2 * bins, LANES):
        for s in range(n_src):
            part = white[s * block : (s + 1) * block, f : f + LANES]
            mixed[f // LANES, pl.ds(s, block, stride=n_src), :] = part
        out[:, f : f + LANES] = mixed[f // LANES].astype(out.dtype)


def whitened_of(plan, table, spare, mine, came):
    n_src, block, length = mine.shape
    width = table.shape[1]
    rows = n_src * block
    return pl.pallas_call(
        functools.partial(whiten_kernel, spare),
        out_shape=jax.ShapeDtypeStruct((rows, width), jnp.bfloat16),
        in_specs=[SMEM] + [VMEM] * (2 + len(came)),
        out_specs=VMEM,
        scratch_shapes=[
            pltpu.VMEM((width // LANES, rows, LANES), jnp.float32),
            pltpu.VMEM((n_src, block, length), mine.dtype),
        ],
        compiler_params=ROOM,
        name="whiten",
    )(plan, table, mine, *came)


def cross_kernel(places, mode, first, spectra, *rest):
    both = mode == "both"
    whites, rest = rest[: len(places)], rest[len(places) :]
    acc, out, conj = (None, *rest) if first else rest
    chans, rec_rows = spectra.shape[1:3]
    width = whites[0].shape[1]
    n_src = out.shape[-2]
    part_rows = rec_rows // (QUAD * STREAMS)
    bins = width // 2
    tiles = bins // LANES
    quad = lax.rem(lax.axis_index("chan"), QUAD)
    core = lax.axis_index("rec")
    part = core if mode == "keep" else 1 - core
    for k, white in enumerate(whites):
        for f in range(tiles):
            real = white[:, f * LANES : (f + 1) * LANES].astype(jnp.float32)
            imag = white[:, bins + f * LANES : bins + (f + 1) * LANES].astype(jnp.float32)
            conj[k, 0, f] = real if both else jnp.where(part == 0, real, -imag)
            conj[k, 1, f] = imag if both else jnp.where(part == 0, imag, real)
    group = 8 if both else chans

    @pl.loop(0, tiles)
    def _(f):
        lo = pl.multiple_of(f * LANES, LANES)
        for c0 in range(0, chans, group):
            names = range(c0, c0 + group)
            if both:
                spots = [(p, c) for c in names for p in (0, 1)]
            else:
                spots = [(part, c) for c in names]
            if first:
                sums = [jnp.zeros((n_src, LANES), jnp.float32) for _ in spots]
            else:
                sums = [acc[p, c, :, pl.ds(lo, LANES)] for p, c in spots]
            for k, (other, stream) in enumerate(places):
                base = ((quad ^ other) * STREAMS + stream) * part_rows
                for r in range(part_rows):
                    a = conj[k, 0, f, r * n_src : (r + 1) * n_src, :]
                    b = conj[k, 1, f, r * n_src : (r + 1) * n_src, :]
                    for i, c in enumerate(names):
                        xr = spectra[f, c, pl.ds(base + r, 1), :]
                        xi = spectra[tiles + f, c, pl.ds(base + r, 1), :]
                        if both:
                            sums[2 * i] += xr * a + xi * b
                            sums[2 * i + 1] += xi * a - xr * b
                        else:
                            sums[i] += xr * a + xi * b
            for (p, c), total in zip(spots, sums):
                if both:
                    out[p, c, :, pl.ds(lo, LANES)] = total
                else:
                    out[c, :, pl.ds(lo, LANES)] = total.astype(out.dtype)


def cross_of(spectra, blocks, n_src, mode="both", acc=None):
    places, whites = zip(*blocks)
    chans = spectra.shape[1]
    rows, width = whites[0].shape
    bins = width // 2
    both = mode == "both"
    shape = (2, chans, n_src, bins) if both else (chans, n_src, bins)
    args = (spectra, *whites) + (() if acc is None else (acc,))
    return pl.pallas_call(
        functools.partial(cross_kernel, places, mode, acc is None),
        out_shape=jax.ShapeDtypeStruct(shape, jnp.bfloat16 if mode == "send" else jnp.float32),
        in_specs=[VMEM] * len(args),
        out_specs=VMEM,
        scratch_shapes=[pltpu.VMEM((len(places), 2, bins // LANES, rows, LANES), jnp.float32)],
        input_output_aliases={len(args) - 1: 0} if both and acc is not None else {},
        cost_estimate=pl.CostEstimate(
            flops=4 * (2 if both else 1) * chans * rows * bins * len(places) * 16,
            bytes_accessed=rows * chans * width * len(places),
            transcendentals=0,
        ),
        compiler_params=ROOM,
    )(*args)


def stacks(records, valid, sources):
    per_dev, rec_rows, length = records.shape
    bins = length // 2
    n_src = sources.shape[0]
    n_chan = lax.axis_size("chan")
    n_rec = lax.axis_size("rec")
    table = dft_table(length, bins)

    def swap(value, bit):
        return lax.ppermute(value, "chan", [(i, i ^ bit) for i in range(n_chan)])

    room = n_src // 2
    picked = pick(sources, valid, records, room)
    first, more = picked[:QUAD], picked[QUAD:]
    came = {j: swap(first[j], j) for j in (3, 1, 2)}
    packed = n_chan == 2 * QUAD
    spare = spare_of(n_src) if packed else 0
    plan = plan_of(sources, per_dev, room, packed)

    def exchange(bits):
        def run(parts):
            return [
                lax.ppermute(x, "chan", [(i, i ^ bit) for i in range(n_chan)])
                for x, bit in zip(parts, bits)
            ]

        return run

    def same(parts):
        return parts

    rest = lax.cond(plan[-2] > 0, exchange((1, 2, 3)), same, list(more[1:]))
    parts = merge(plan, n_src, spare, [first[0], came[1], came[2], came[3], more[0], *rest])
    homes, sent, left = parts[:STREAMS], parts[STREAMS : 2 * STREAMS], parts[2 * STREAMS :]
    last = n_chan // 2
    others = []
    if packed:
        for t in range(STREAMS):
            others.append([swap(sent[t], last)])
        left = lax.cond(plan[-1] > 0, exchange((last,) * STREAMS), same, list(left))
        *left, valid = lax.optimization_barrier((*left, valid))
        for t in range(STREAMS):
            others[t].append(left[t])
    else:
        homes = list(homes)
        for t in range(STREAMS):
            bit = QUAD
            while bit < last:
                homes[t] = homes[t] + swap(homes[t], bit)
                bit *= 2
            others.append([swap(homes[t], last)])
    spectra = spectra_of(valid, table, records)
    acc = None
    gathered = []
    for t in range(STREAMS):
        white = whitened_of(plan, table, spare, homes[t], others[t])
        blocks = [((0, t), white)]
        for j in (3, 1, 2):
            blocks.append(((j, t), swap(white, j)))
        gathered.append(blocks)
        acc = cross_of(spectra, gathered[t][:1], n_src, "both", acc)
    for t in range(STREAMS):
        mine, *near, far = gathered[t]
        for block in near:
            acc = cross_of(spectra, [block], n_src, "both", acc)
        if t < STREAMS - 1:
            acc = cross_of(spectra, [far], n_src, "both", acc)
    send = cross_of(spectra, [far], n_src, "send", acc)
    came = lax.ppermute(send, "rec", [(i, i ^ 1) for i in range(n_rec)])
    keep = cross_of(spectra, [far], n_src, "keep", acc)
    return (keep + came.astype(jnp.float32)) / (rec_rows * n_rec)


def solution(mesh):
    placed = (P(("group", "chan"), "rec", None), P(("group", "chan"), "rec"), P("group"))
    return jax.shard_map(
        stacks,
        mesh=mesh,
        in_specs=placed,
        out_specs=P(("group", "chan"), None, "rec"),
        check_vma=False,
    )
```
